32 devices in a mesh: layer: 8 (over z, x), dp: 4 (over y, core).
Axes of the slice: x: 2, y: 2, z: 4, core: 2. Of those that a mesh axis runs over, the one named last changes fastest.
Arguments:
- old_heads: float32 [8, 1024, 512], P('layer', 'dp'), parts along dimension 1, may hold values from -6 to 6
- surrogate: float32 [8, 512, 512], P('layer'), may hold values from -0.25 to 0.25
- norm_gain: float32 [8, 512], P('layer'), may hold values from 0.25 to 1.75
- w_qkv: bfloat16 [8, 512, 1536], P('layer'), may hold values from -16 to 16
- w_out: bfloat16 [8, 512, 512], P('layer'), may hold values from -0.25 to 0.25
- w_up: bfloat16 [8, 512, 2048], P('layer'), may hold values from -0.25 to 0.25
- w_down: bfloat16 [8, 2048, 512], P('layer'), may hold values from -0.125 to 0.125
- lengths: int32 [8], P('dp'), parts along dimension 0, may hold values from 32 to 128
Outputs:
- new_heads: float32 [8, 1024, 512], P('layer', 'dp'), parts along dimension 1
- update_rms: float32 [8, 1024], P('layer', 'dp'), parts along dimension 1
The draws below stay inside these ranges and needn't reach their ends.
There are 4 independent parts, one for each index of `dp`. The reference program is written for one: setup_inputs(seed, part) draws one part's arguments, and reference() takes and returns one part's arrays. A program takes and returns all parts, laid end to end along the dimension named above; an argument that names none is the same for every part. Nothing has to cross between parts.
All inputs are finite; a program needn't handle non-finite values.
Results may differ from the reference program's by a relative error of at most 0.015.
Values sent between devices are 32-bit elements; how exact they have to be, the bound alone decides.
No kernel may reach another device: no remote copies, remote signals or barrier semaphores. Data moves between devices by JAX's collectives and lax.ppermute only.
A program may use at most 128 MiB of HBM per device.

```python
import math
import jax
import jax.numpy as jnp
from jax import lax

D = 512
FF = 2048
HEAD_DIM = 64
SEQ = 128
FINE = 4
SEQS = 2
TOKENS = 256
LAYERS = 8


def draw_w_qkv(key, part):
    base = jax.random.truncated_normal(key, -4.0, 4.0, (LAYERS, D, 3 * D), jnp.float32) * D ** (-0.5)
    return base.astype(jnp.bfloat16)


def steps_of(rng, dims, pieces, smallest, high):
    level = 1.0
    for axis_at, shards_of in pieces:
        draws = jax.random.uniform(jax.random.fold_in(jax.random.fold_in(rng, 6), axis_at), (shards_of,), jnp.float32, smallest / len(pieces), high / len(pieces))
        level = level * jnp.repeat(jnp.exp(draws), dims[axis_at] // shards_of).reshape((-1,) + (1,) * (len(dims) - 1 - axis_at))
    return level


def scatter_about(own_key, extent, spread, limit, split=(), kind=jnp.bfloat16):
    factor_of = steps_of(own_key, extent, split, -0.22, 0.18) if split else 1.0
    values = jax.random.normal(own_key, extent, jnp.float32) * spread * factor_of
    return jnp.minimum(jnp.maximum(values, -limit), limit).astype(kind)


def setup_inputs(seed: int = 0, part: int = 0) -> dict:
    arg_keys = jax.random.split(jax.random.key(seed), 9)
    part_splits = jax.random.split(jax.random.fold_in(arg_keys[8], part), 9)
    old_heads = scatter_about(part_splits[0], (LAYERS, TOKENS, D), 1.0, 6.0, ((0, 8),), jnp.float32)
    surrogate = scatter_about(arg_keys[1], (LAYERS, D, D), D ** -0.5, 0.25, ((0, 8),), jnp.float32)
    norm_gain = jnp.clip(1.0 + 0.15 * jax.random.normal(arg_keys[2], (LAYERS, D), jnp.float32), 0.25, 1.75)
    w_qkv = draw_w_qkv(jax.random.fold_in(arg_keys[8], 71), part)
    w_out = scatter_about(arg_keys[4], (LAYERS, D, D), D ** -0.5, 0.25, ((0, 8),))
    w_up = scatter_about(arg_keys[5], (LAYERS, D, FF), D ** -0.5, 0.25, ((0, 8),))
    w_down = scatter_about(arg_keys[6], (LAYERS, FF, D), FF ** -0.5, 0.125, ((0, 8),))
    lengths = jax.random.randint(part_splits[7], (SEQS,), SEQ // 4, SEQ + 1).astype(jnp.int32)
    return {"old_heads": old_heads, "surrogate": surrogate, "norm_gain": norm_gain, "w_qkv": w_qkv, "w_out": w_out, "w_up": w_up, "w_down": w_down, "lengths": lengths}


precise = lax.Precision.HIGHEST

def causal_allowed(lengths):
    position = jnp.arange(SEQ, dtype=jnp.int32)
    ordered = position[None, :, None] >= position[None, None, :]
    inside = position[None, None, :] < lengths[:, None, None]
    return ordered & inside

def layer_step(current, gain_row, w_qkv, w_out, w_up, w_down, allowed):
    mean_square = lax.optimization_barrier(jnp.mean(current * current, axis=1, keepdims=True))
    normed = (current * lax.rsqrt(mean_square + 1e-06) * gain_row).astype(jnp.bfloat16)
    packed = jnp.dot(normed, w_qkv, preferred_element_type=jnp.float32).astype(jnp.bfloat16)
    model_width = normed.shape[1]
    head_count = model_width // HEAD_DIM

    def split_heads(block):
        return block.reshape(SEQS, SEQ, head_count, HEAD_DIM).astype(jnp.float32)
    queries = split_heads(packed[:, :model_width])
    key_heads = split_heads(packed[:, model_width:2 * model_width])
    values = split_heads(packed[:, 2 * model_width:])
    scores = jnp.einsum('sqhd,skhd->shqk', queries, key_heads) / math.sqrt(HEAD_DIM)
    scores = jnp.where(allowed[:, None], scores, -1e+30)
    row_max = lax.optimization_barrier(jnp.max(scores, axis=-1, keepdims=True))
    exponent = jnp.exp(scores - row_max)
    attention = (exponent / lax.optimization_barrier(jnp.sum(exponent, axis=-1, keepdims=True))).astype(jnp.bfloat16)
    mixed_heads = jnp.einsum('shqk,skhd->sqhd', attention.astype(jnp.float32), values)
    mixed_heads = mixed_heads.astype(jnp.bfloat16).reshape(SEQS * SEQ, model_width)
    attended = jnp.dot(mixed_heads, w_out, preferred_element_type=jnp.float32)
    hidden = jax.nn.gelu(jnp.dot(normed, w_up, preferred_element_type=jnp.float32), approximate=True).astype(jnp.bfloat16)
    return attended + jnp.dot(hidden, w_down, preferred_element_type=jnp.float32)

def fine_sweep(own_start, gain_row, w_qkv, w_out, w_up, w_down, allowed):
    current = own_start
    for substep in range(FINE):
        current = current + layer_step(current, gain_row, w_qkv, w_out, w_up, w_down, allowed) * (1.0 / FINE)
    return current

def reference(old_heads, surrogate, norm_gain, w_qkv, w_out, w_up, w_down, lengths):
    allowed = causal_allowed(lengths)
    identity = jnp.eye(D, dtype=jnp.float32)

    def advance(previous, layer_inputs):
        own_start, surrogate_row, gain_row, qkv_row, out_row, up_row, down_row, layer_index = layer_inputs
        fine_end = fine_sweep(own_start, gain_row, qkv_row, out_row, up_row, down_row, allowed)
        coarse = 0.9 * identity + 0.3 * surrogate_row
        jump_term = fine_end - jnp.dot(own_start, coarse, precision=precise, preferred_element_type=jnp.float32)
        chained = jnp.dot(previous, coarse, precision=precise, preferred_element_type=jnp.float32) + jump_term
        produced = jnp.where(layer_index == 0, fine_end, chained)
        difference = previous - own_start
        change = jnp.sqrt(lax.optimization_barrier(jnp.mean(difference * difference, axis=1)))
        return (produced, (produced, change))
    layer_ids = jnp.arange(LAYERS, dtype=jnp.int32)
    final_state, outputs = lax.scan(advance, old_heads[0], (old_heads, surrogate, norm_gain, w_qkv, w_out, w_up, w_down, layer_ids))
    return (outputs[0], outputs[1])
```

```python
import functools
import math

import jax
import jax.numpy as jnp
from jax import lax
from jax.experimental import pallas as pl
from jax.experimental.pallas import tpu as pltpu
from jax.sharding import PartitionSpec as P

HEAD_DIM = 64
SEQ = 128
FINE = 4
PAIR = 2 * HEAD_DIM
F32 = jnp.float32
BF16 = jnp.bfloat16


def halves_of(a):
    high = a.astype(BF16)
    return high, (a - high.astype(F32)).astype(BF16)


def dot3(a, b):
    a_high, a_low = halves_of(a)
    b_high, b_low = halves_of(b)
    dot = functools.partial(jnp.dot, preferred_element_type=F32)
    return dot(a_high, b_high) + (dot(a_low, b_high) + dot(a_high, b_low))


def coarse_of(a, varying):
    return 0.9 * a + 0.3 * dot3(a, varying)


def in_vmem():
    return pl.BlockSpec(memory_space=pltpu.VMEM)


def in_smem():
    return pl.BlockSpec(memory_space=pltpu.SMEM)


def in_place():
    return pl.BlockSpec(memory_space=pl.ANY)


def fine_kernel(
    position, lengths, start, gain, surrogate, w_qkv, w_out, w_up, w_down,
    kept, sent,
    w_in, w_back, varying, state, act, qkv, bias, sems,
):
    tokens, width = state.shape
    hidden = w_back.shape[0] - width
    copies = [
        pltpu.make_async_copy(w_qkv.at[0], w_in.at[:, pl.ds(0, 3 * width)], sems.at[0]),
        pltpu.make_async_copy(w_up.at[0], w_in.at[:, pl.ds(3 * width, hidden)], sems.at[1]),
        pltpu.make_async_copy(w_out.at[0], w_back.at[pl.ds(0, width), :], sems.at[2]),
        pltpu.make_async_copy(w_down.at[0], w_back.at[pl.ds(width, hidden), :], sems.at[3]),
        pltpu.make_async_copy(surrogate.at[0], varying, sems.at[4]),
    ]
    for copy in copies:
        copy.start()
    state[...] = start[0]
    query = lax.broadcasted_iota(jnp.int32, (SEQ, SEQ), 0)
    key = lax.broadcasted_iota(jnp.int32, (SEQ, SEQ), 1)
    sequences = tokens // SEQ
    for s in range(sequences):
        allowed = (key <= query) & (key < lengths[s])
        bias[pl.ds(s * SEQ, SEQ), :] = jnp.where(allowed, 0.0, -1e30).astype(F32)
    for copy in copies:
        copy.wait()
    low = lax.broadcasted_iota(jnp.int32, (SEQ, PAIR), 1) < HEAD_DIM
    zeros = jnp.zeros((SEQ, PAIR), BF16)
    ones = jnp.ones((SEQ, PAIR), BF16)

    def by_head(block):
        return jnp.concatenate([jnp.where(low, block, zeros), jnp.where(low, zeros, block)], 0)

    counts = by_head(ones)
    chunk = width
    curve = math.sqrt(2 / math.pi)

    def substep(_, carry):
        x = state[...]
        mean_square = jnp.mean(x * x, axis=1, keepdims=True)
        normed = (x * lax.rsqrt(mean_square + 1e-06) * gain[...]).astype(BF16)
        for n in range(0, 3 * width, chunk):
            packed = jnp.dot(normed, w_in[:, n : n + chunk], preferred_element_type=F32).astype(BF16)
            if n < width:
                packed = packed * jnp.asarray(1 / math.sqrt(HEAD_DIM), BF16)
            qkv[:, n : n + chunk] = packed
        for s in range(sequences):
            rows = pl.ds(s * SEQ, SEQ)
            mask = bias[rows, :]
            masks = jnp.concatenate([mask, mask], 0)
            for at in range(0, width, PAIR):
                queries = qkv[rows, at : at + PAIR]
                keys = qkv[rows, width + at : width + at + PAIR]
                values = qkv[rows, 2 * width + at : 2 * width + at + PAIR]
                scores = lax.dot_general(
                    by_head(queries), keys, (((1,), (1,)), ((), ())), preferred_element_type=F32
                ) + masks
                top = jnp.max(scores, axis=-1, keepdims=True)
                weights = jnp.exp(scores - top).astype(BF16)
                pair = jnp.concatenate([weights[:SEQ], weights[SEQ:]], 1)
                both = jnp.dot(
                    pair, jnp.concatenate([by_head(values), counts], 1), preferred_element_type=F32
                )
                act[rows, at : at + PAIR] = (both[:, :PAIR] / both[:, PAIR:]).astype(BF16)
        for n in range(0, hidden, chunk):
            u = jnp.dot(
                normed, w_in[:, 3 * width + n : 3 * width + n + chunk], preferred_element_type=F32
            )
            half = 0.5 * u
            gelu = half + half * jnp.tanh(u * (curve + (curve * 0.044715) * (u * u)))
            act[:, width + n : width + n + chunk] = gelu.astype(BF16)
        state[...] = x + jnp.dot(act[...], w_back[...], preferred_element_type=F32) * (1.0 / FINE)
        return carry

    lax.fori_loop(0, FINE, substep, 0)
    begun = start[0]
    share = jnp.where(position[0] == 0, 0.0, 1.0).astype(F32)
    state[...] = state[...] - share * coarse_of(begun, varying[...])
    half_rows = tokens // 2
    mine = position[0] % 2
    kept[...] = state[pl.ds(pl.multiple_of(mine * half_rows, half_rows), half_rows), :]
    sent[...] = state[pl.ds(pl.multiple_of((1 - mine) * half_rows, half_rows), half_rows), :]


def fine_jump(position, lengths, start, gain, surrogate, w_qkv, w_out, w_up, w_down):
    tokens, width = start.shape[1:]
    hidden = w_up.shape[2]
    half = jax.ShapeDtypeStruct((tokens // 2, width), F32)
    return pl.pallas_call(
        fine_kernel,
        in_specs=[in_smem(), in_smem(), in_vmem(), in_vmem()] + [in_place()] * 5,
        out_specs=[in_vmem()] * 2,
        out_shape=[half, half],
        scratch_shapes=[
            pltpu.VMEM((width, 3 * width + hidden), BF16),
            pltpu.VMEM((width + hidden, width), BF16),
            pltpu.VMEM((width, width), F32),
            pltpu.VMEM((tokens, width), F32),
            pltpu.VMEM((tokens, width + hidden), BF16),
            pltpu.VMEM((tokens, 3 * width), BF16),
            pltpu.VMEM((tokens, SEQ), F32),
            pltpu.SemaphoreType.DMA((5,)),
        ],
    )(position, lengths, start, gain, surrogate, w_qkv, w_out, w_up, w_down)


def hop_kernel(position, incoming, kept, received, own, other, out):
    def over(first_jump, first, second_jump, second):
        middle = first_jump + coarse_of(incoming[...], first)
        out[...] = second_jump + coarse_of(middle, second)

    even = position[0] % 2 == 0

    @pl.when(even)
    def _():
        over(kept[...], own[...], received[...], other[...])

    @pl.when(jnp.logical_not(even))
    def _():
        over(received[...], other[...], kept[...], own[...])


def hop(position, incoming, kept, received, own, other):
    return pl.pallas_call(
        hop_kernel,
        in_specs=[in_smem()] + [in_vmem()] * 5,
        out_specs=in_vmem(),
        out_shape=jax.ShapeDtypeStruct(incoming.shape, F32),
    )(position, incoming, kept, received, own, other)


def turn_kernel(position, incoming, kept, own, received_jump, other, head, out):
    even = position[0] % 2 == 0

    @pl.when(even)
    def _():
        head[...] = incoming[...]
        out[...] = kept[...] + coarse_of(incoming[...], own[...])

    @pl.when(jnp.logical_not(even))
    def _():
        head[...] = received_jump[...] + coarse_of(incoming[...], other[...])
        out[...] = incoming[...]


def turn(position, incoming, kept, own, received, other):
    shape = jax.ShapeDtypeStruct(incoming.shape, F32)
    return pl.pallas_call(
        turn_kernel,
        in_specs=[in_smem()] + [in_vmem()] * 5,
        out_specs=[in_vmem()] * 2,
        out_shape=[shape, shape],
    )(position, incoming, kept, own, received, other)


def close_kernel(position, head, returned, kept, sent, own, start, out, change):
    half = head.shape[0]
    width = head.shape[1]
    share = jnp.where(position[0] == 0, 0.0, 1.0).astype(F32)
    for at, ahead, jump in ((0, head, kept), (1, returned, sent)):
        where = (position[0] % 2 + at) % 2
        rows = pl.ds(pl.multiple_of(where * half, half), half)
        state = share * ahead[...]
        out[0, rows, :] = jump[...] + coarse_of(state, own[...])
        difference = ahead[...] - start[0, rows, :]
        total = lax.dot_general(
            jnp.ones((8, width), F32), difference * difference, (((1,), (1,)), ((), ())),
            precision=lax.Precision.HIGHEST, preferred_element_type=F32,
        )
        change[:, rows] = share * jnp.sqrt(total[:1] * (1.0 / width))


def close(position, head, returned, kept, sent, own, start):
    tokens, width = start.shape[1:]
    return pl.pallas_call(
        close_kernel,
        in_specs=[in_smem()] + [in_vmem()] * 6,
        out_specs=[in_vmem()] * 2,
        out_shape=[
            jax.ShapeDtypeStruct((1, tokens, width), F32),
            jax.ShapeDtypeStruct((1, tokens), F32),
        ],
    )(position, head, returned, kept, sent, own, start)


def shards(old_heads, surrogate, norm_gain, w_qkv, w_out, w_up, w_down, lengths):
    layers = lax.axis_size("layer")
    batches = lax.axis_size("dp")
    layer = lax.axis_index("layer")
    batch = lax.axis_index("dp")
    position = layer.astype(jnp.int32).reshape(1)
    partners = [(i, i ^ 1) for i in range(layers)]
    neighbours = [(i, i ^ 1) for i in range(batches)]

    width = surrogate.shape[1]
    part = width // 2
    mine = lax.dynamic_slice_in_dim(surrogate[0], (batch % 2) * part, part, 0)
    got = lax.ppermute(mine, "layer", partners)
    passed = lax.ppermute(got, "dp", neighbours)
    first = batch % 2 == 0
    other = jnp.concatenate([jnp.where(first, got, passed), jnp.where(first, passed, got)], 0)
    own = surrogate[0]

    kept, sent = fine_jump(
        position, lengths, old_heads, norm_gain, surrogate, w_qkv, w_out, w_up, w_down
    )
    received = lax.ppermute(sent, "layer", partners)
    arrived = jnp.zeros_like(kept)
    incoming = arrived
    for at in range(0, layers - 2, 2):
        carried = hop(position, incoming, kept, received, own, other)
        incoming = lax.ppermute(carried, "layer", [(at, at + 2), (at + 1, at + 3)])
        arrived = arrived + incoming
    head, out = turn(position, arrived, kept, own, received, other)
    returned = lax.ppermute(out, "layer", partners)
    return close(position, head, returned, kept, sent, own, old_heads)


def solution(mesh):
    in_specs = (
        P("layer", "dp", None),
        P("layer", None, None),
        P("layer", None),
        P("layer", None, None),
        P("layer", None, None),
        P("layer", None, None),
        P("layer", None, None),
        P("dp"),
    )
    out_specs = (P("layer", "dp", None), P("layer", "dp"))
    return jax.shard_map(shards, mesh=mesh, in_specs=in_specs, out_specs=out_specs, check_vma=False)
```

```python
import functools
import math

import jax
import jax.numpy as jnp
from jax import lax
from jax.experimental import pallas as pl
from jax.experimental.pallas import tpu as pltpu
from jax.sharding import PartitionSpec as P


HEAD_DIM = 64
SEQ = 128
FINE = 4
CHUNKS = 2
PAIR = 2 * HEAD_DIM
F32 = jnp.float32
BF16 = jnp.bfloat16


def halves_of(a):
    high = a.astype(BF16)
    return high, (a - high.astype(F32)).astype(BF16)


def dot3(a, b):
    a_high, a_low = halves_of(a)
    b_high, b_low = halves_of(b)
    dot = functools.partial(jnp.dot, preferred_element_type=F32)
    return dot(a_high, b_high) + (dot(a_low, b_high) + dot(a_high, b_low))


def dot_split(a, b_high, b_low):
    a_high, a_low = halves_of(a)
    rows = a.shape[0]
    both = jnp.dot(jnp.concatenate([a_high, a_low], 0), b_high, preferred_element_type=F32)
    return both[:rows] + (both[rows:] + jnp.dot(a_high, b_low, preferred_element_type=F32))


def params(megabytes):
    return pltpu.CompilerParams(vmem_limit_bytes=megabytes << 20)


def in_vmem():
    return pl.BlockSpec(memory_space=pltpu.VMEM)


def in_smem():
    return pl.BlockSpec(memory_space=pltpu.SMEM)


def in_place():
    return pl.BlockSpec(memory_space=pltpu.HBM)


def fine_kernel(
    position, lengths, start, gain, surrogate, w_qkv, w_out, w_up, w_down, *outs_and_scratch
):
    *pieces, w_in, w_back, varying, state, act, qkv, bias, sems = outs_and_scratch
    tokens, width = state.shape
    hidden = w_back.shape[0] - width
    copies = [
        pltpu.make_async_copy(w_qkv.at[0], w_in.at[:, pl.ds(0, 3 * width)], sems.at[0]),
        pltpu.make_async_copy(w_up.at[0], w_in.at[:, pl.ds(3 * width, hidden)], sems.at[1]),
        pltpu.make_async_copy(w_out.at[0], w_back.at[pl.ds(0, width), :], sems.at[2]),
        pltpu.make_async_copy(w_down.at[0], w_back.at[pl.ds(width, hidden), :], sems.at[3]),
        pltpu.make_async_copy(surrogate.at[0], varying, sems.at[4]),
    ]
    for copy in copies:
        copy.start()
    state[...] = start[0]
    query = lax.broadcasted_iota(jnp.int32, (SEQ, SEQ), 0)
    key = lax.broadcasted_iota(jnp.int32, (SEQ, SEQ), 1)
    sequences = tokens // SEQ
    for s in range(sequences):
        allowed = (key <= query) & (key < lengths[s])
        bias[pl.ds(s * SEQ, SEQ), :] = jnp.where(allowed, 0.0, -1e30).astype(F32)
    for copy in copies:
        copy.wait()
    low = lax.broadcasted_iota(jnp.int32, (SEQ, PAIR), 1) < HEAD_DIM
    zeros = jnp.zeros((SEQ, PAIR), BF16)
    ones = jnp.ones((SEQ, PAIR), BF16)

    def by_head(block):
        return jnp.concatenate([jnp.where(low, block, zeros), jnp.where(low, zeros, block)], 0)

    counts = by_head(ones)
    chunk = width
    curve = math.sqrt(2 / math.pi)

    def substep(_, carry):
        x = state[...]
        mean_square = jnp.mean(x * x, axis=1, keepdims=True)
        normed = (x * lax.rsqrt(mean_square + 1e-06) * gain[...]).astype(BF16)
        for n in range(0, 3 * width, chunk):
            packed = jnp.dot(normed, w_in[:, n : n + chunk], preferred_element_type=F32).astype(BF16)
            if n < width:
                packed = packed * jnp.asarray(1 / math.sqrt(HEAD_DIM), BF16)
            qkv[:, n : n + chunk] = packed
        for s in range(sequences):
            rows = pl.ds(s * SEQ, SEQ)
            mask = bias[rows, :]
            masks = jnp.concatenate([mask, mask], 0)
            for at in range(0, width, PAIR):
                queries = qkv[rows, at : at + PAIR]
                keys = qkv[rows, width + at : width + at + PAIR]
                values = qkv[rows, 2 * width + at : 2 * width + at + PAIR]
                scores = lax.dot_general(
                    by_head(queries), keys, (((1,), (1,)), ((), ())), preferred_element_type=F32
                ) + masks
                top = jnp.max(scores, axis=-1, keepdims=True)
                weights = jnp.exp(scores - top).astype(BF16)
                pair = jnp.concatenate([weights[:SEQ], weights[SEQ:]], 1)
                both = jnp.dot(
                    pair, jnp.concatenate([by_head(values), counts], 1), preferred_element_type=F32
                )
                act[rows, at : at + PAIR] = (both[:, :PAIR] / both[:, PAIR:]).astype(BF16)
        for n in range(0, hidden, chunk):
            u = jnp.dot(
                normed, w_in[:, 3 * width + n : 3 * width + n + chunk], preferred_element_type=F32
            )
            half = 0.5 * u
            gelu = half + half * jnp.tanh(u * (curve + (curve * 0.044715) * (u * u)))
            act[:, width + n : width + n + chunk] = gelu.astype(BF16)
        state[...] = x + jnp.dot(act[...], w_back[...], preferred_element_type=F32) * (1.0 / FINE)
        return carry

    lax.fori_loop(0, FINE, substep, 0)
    begun = start[0]
    share = jnp.where(position[0] == 0, 0.0, 1.0).astype(F32)
    state[...] = state[...] - share * (0.9 * begun + 0.3 * dot3(begun, varying[...]))
    mine = position[0] % 2
    half = pieces[0].shape[0]
    for at in range(len(pieces) // 2):
        for piece, part in ((pieces[2 * at], mine), (pieces[2 * at + 1], 1 - mine)):
            piece[...] = state[pl.ds(pl.multiple_of((2 * at + part) * half, half), half), :]


def fine_jump(chunks, position, lengths, start, gain, surrogate, w_qkv, w_out, w_up, w_down):
    tokens, width = start.shape[1:]
    hidden = w_up.shape[2]
    half = jax.ShapeDtypeStruct((tokens // (2 * chunks), width), F32)
    return pl.pallas_call(
        fine_kernel,
        in_specs=[in_smem(), in_smem(), in_vmem(), in_vmem()] + [in_place()] * 5,
        out_specs=[in_vmem()] * (2 * chunks),
        out_shape=[half] * (2 * chunks),
        scratch_shapes=[
            pltpu.VMEM((width, 3 * width + hidden), BF16),
            pltpu.VMEM((width + hidden, width), BF16),
            pltpu.VMEM((width, width), F32),
            pltpu.VMEM((tokens, width), F32),
            pltpu.VMEM((tokens, width + hidden), BF16),
            pltpu.VMEM((tokens, 3 * width), BF16),
            pltpu.VMEM((tokens, SEQ), F32),
            pltpu.SemaphoreType.DMA((5,)),
        ],
        cost_estimate=pl.CostEstimate(
            flops=2 * FINE * tokens * width * (4 * width + 2 * hidden),
            transcendentals=FINE * tokens * hidden,
            bytes_accessed=2 * width * (4 * width + 2 * hidden),
        ),
        compiler_params=params(62),
    )(position, lengths, start, gain, surrogate, w_qkv, w_out, w_up, w_down)


def maps_kernel(
    parity, own, got, passed,
    own_high, own_low, even_high, even_low, odd_high, odd_low, both_high, both_low, even, odd,
):
    part = got.shape[0]
    flag, core = parity[0], parity[1]

    def place(other):
        for source, where in ((got, core), (passed, 1 - core)):
            other[pl.ds(pl.multiple_of(where * part, part), part), :] = 0.3 * source[...]

    mine = 0.3 * own[0]
    own_high[...], own_low[...] = halves_of(mine)

    @pl.when(flag == 0)
    def _():
        even[...] = mine
        place(odd)

    @pl.when(flag != 0)
    def _():
        odd[...] = mine
        place(even)

    first, second = even[...], odd[...]
    even_high[...], even_low[...] = halves_of(first)
    odd_high[...], odd_low[...] = halves_of(second)
    product = 0.9 * (first + second) + dot_split(first, odd_high[...], odd_low[...])
    both_high[...], both_low[...] = halves_of(product)


def maps(parity, own, got, passed):
    width = own.shape[1]
    square = jax.ShapeDtypeStruct((width, width), BF16)
    return pl.pallas_call(
        maps_kernel,
        in_specs=[in_smem()] + [in_vmem()] * 3,
        out_specs=[in_vmem()] * 8,
        out_shape=[square] * 8,
        scratch_shapes=[pltpu.VMEM((width, width), F32)] * 2,
        compiler_params=params(16),
    )(parity, own, got, passed)


def join_kernel(parity, kept, received, odd_high, odd_low, out):
    even = parity[0] == 0
    first = jnp.where(even, kept[...], received[...])
    second = jnp.where(even, received[...], kept[...])
    out[...] = second + (0.9 * first + dot_split(first, odd_high[...], odd_low[...]))


def join(parity, kept, received, odd):
    return pl.pallas_call(
        join_kernel,
        in_specs=[in_smem()] + [in_vmem()] * 4,
        out_specs=in_vmem(),
        out_shape=jax.ShapeDtypeStruct(kept.shape, F32),
        compiler_params=params(8),
    )(parity, kept, received, *odd)


def hop_kernel(incoming, joined, both_high, both_low, out):
    state = incoming[...]
    out[...] = joined[...] + (0.81 * state + dot_split(state, both_high[...], both_low[...]))


def hop(incoming, joined, both):
    return pl.pallas_call(
        hop_kernel,
        in_specs=[in_vmem()] * 4,
        out_specs=in_vmem(),
        out_shape=jax.ShapeDtypeStruct(incoming.shape, F32),
        compiler_params=params(8),
    )(incoming, joined, *both)


def turn_kernel(parity, kept, received, even_high, even_low, *arrivals_and_outs):
    *arrivals, head, out = arrivals_and_outs
    state = functools.reduce(jnp.add, [arrival[...] for arrival in arrivals])
    even = parity[0] == 0
    first = jnp.where(even, kept[...], received[...])
    after = first + (0.9 * state + dot_split(state, even_high[...], even_low[...]))
    head[...] = jnp.where(even, state, after)
    out[...] = jnp.where(even, after, state)


def turn(parity, kept, received, even, arrivals):
    shape = jax.ShapeDtypeStruct(kept.shape, F32)
    return pl.pallas_call(
        turn_kernel,
        in_specs=[in_smem()] + [in_vmem()] * (4 + len(arrivals)),
        out_specs=[in_vmem()] * 2,
        out_shape=[shape, shape],
        compiler_params=params(8),
    )(parity, kept, received, *even, *arrivals)


def close_kernel(chunks, position, start, own_high, own_low, *rest):
    *pieces, out, change = rest
    half, _ = pieces[0].shape
    share = jnp.where(position[0] == 0, 0.0, 1.0).astype(F32)
    for at in range(chunks):
        head, returned, kept, sent = pieces[4 * at : 4 * at + 4]
        for ahead, jump, other in ((head, kept, 0), (returned, sent, 1)):
            where = (position[0] + other) % 2 + 2 * at
            rows = pl.ds(pl.multiple_of(where * half, half), half)
            state = share * ahead[...]
            out[0, rows, :] = jump[...] + (
                0.9 * state + dot_split(state, own_high[...], own_low[...])
            )
            difference = state - share * start[0, rows, :]
            mean = jnp.mean(difference * difference, axis=1, keepdims=True)
            change[rows, :] = jnp.broadcast_to(jnp.sqrt(mean), (half, change.shape[1]))


def close(position, start, own, pieces):
    tokens, width = start.shape[1:]
    return pl.pallas_call(
        functools.partial(close_kernel, len(pieces) // 4),
        in_specs=[in_smem()] + [in_vmem()] * (3 + len(pieces)),
        out_specs=[in_vmem()] * 2,
        out_shape=[
            jax.ShapeDtypeStruct((1, tokens, width), F32),
            jax.ShapeDtypeStruct((tokens, 128), F32),
        ],
        compiler_params=params(12),
    )(position, start, *own, *pieces)


def shards(old_heads, surrogate, norm_gain, w_qkv, w_out, w_up, w_down, lengths):
    layers = lax.axis_size("layer")
    batches = lax.axis_size("dp")
    layer = lax.axis_index("layer").astype(jnp.int32)
    core = lax.axis_index("dp").astype(jnp.int32) % 2
    position = layer.reshape(1)
    parity = jnp.stack([layer % 2, core])
    partners = [(i, i ^ 1) for i in range(layers)]
    neighbours = [(i, i ^ 1) for i in range(batches)]

    part = surrogate.shape[1] // 2
    mine = lax.dynamic_slice_in_dim(surrogate[0], core * part, part, 0)
    got = lax.ppermute(mine, "layer", partners)
    pieces = fine_jump(
        CHUNKS, position, lengths, old_heads, norm_gain, surrogate, w_qkv, w_out, w_up, w_down
    )
    passed = lax.ppermute(got, "dp", neighbours)
    kept, sent = pieces[::2], pieces[1::2]
    received = [lax.ppermute(piece, "layer", partners) for piece in sent]
    split = maps(parity, surrogate, got, passed)
    own, even, odd, both = split[0:2], split[2:4], split[4:6], split[6:8]
    spans = range(CHUNKS)
    joined = [join(parity, kept[c], received[c], odd) for c in spans]
    carried = joined
    arrivals = [[] for c in spans]
    for at in range(0, layers - 2, 2):
        route = [(at, at + 2), (at + 1, at + 3)]
        for c in spans:
            arrivals[c].append(lax.ppermute(carried[c], "layer", route))
        if at < layers - 4:
            carried = [hop(arrivals[c][-1], joined[c], both) for c in spans]
    pieces = []
    for c in spans:
        head, out = turn(parity, kept[c], received[c], even, arrivals[c])
        pieces += [head, lax.ppermute(out, "layer", partners), kept[c], sent[c]]
    new_heads, change = close(position, old_heads, own, pieces)
    return new_heads, change[:, :1].reshape(1, -1)


def solution(mesh):
    in_specs = (
        P("layer", "dp", None),
        P("layer", None, None),
        P("layer", None),
        P("layer", None, None),
        P("layer", None, None),
        P("layer", None, None),
        P("layer", None, None),
        P("dp"),
    )
    out_specs = (P("layer", "dp", None), P("layer", "dp"))
    return jax.shard_map(shards, mesh=mesh, in_specs=in_specs, out_specs=out_specs, check_vma=False)
```

```python
import functools
import math

import jax
import jax.numpy as jnp
from jax import lax
from jax.experimental import pallas as pl
from jax.experimental.pallas import tpu as pltpu
from jax.sharding import PartitionSpec as P


HEAD_DIM = 64
SEQ = 128
FINE = 4
QUERY_SCALE = math.log2(math.e) / math.sqrt(HEAD_DIM)
CHUNKS = 2
PAIR = 2 * HEAD_DIM
F32 = jnp.float32
BF16 = jnp.bfloat16


def halves_of(a):
    high = a.astype(BF16)
    return high, (a - high.astype(F32)).astype(BF16)


def dot_split(a, b_high, b_low):
    a_high, a_low = halves_of(a)
    rows = a.shape[0]
    both = jnp.dot(jnp.concatenate([a_high, a_low], 0), b_high, preferred_element_type=F32)
    return both[:rows] + (both[rows:] + jnp.dot(a_high, b_low, preferred_element_type=F32))


def params(megabytes):
    return pltpu.CompilerParams(vmem_limit_bytes=megabytes << 20)


def in_vmem():
    return pl.BlockSpec(memory_space=pltpu.VMEM)


def in_place():
    return pl.BlockSpec(memory_space=pltpu.HBM)


def place():
    return lax.axis_index("layer"), lax.axis_index("dp") % 2


def is_even():
    return lax.axis_index("layer") % 2 == 0


def fine_kernel(
    lengths, start, gain, surrogate, w_qkv, w_out, w_up, w_down, *outs_and_scratch
):
    *pieces, begun, scale, limits, w_in, w_back, varying, state, act, qkv, bias, sems = outs_and_scratch
    tokens, width = state.shape
    hidden = w_back.shape[0] - width
    moves = (
        (start.at[0], begun),
        (gain, scale),
        (w_qkv.at[0], w_in.at[:, pl.ds(0, 3 * width)]),
        (lengths, limits),
        (w_up.at[0], w_in.at[:, pl.ds(3 * width, hidden)]),
        (w_out.at[0], w_back.at[pl.ds(0, width), :]),
        (w_down.at[0], w_back.at[pl.ds(width, hidden), :]),
        (surrogate.at[0], varying),
    )
    copies = [
        pltpu.make_async_copy(source, target, sems.at[at])
        for at, (source, target) in enumerate(moves)
    ]
    for copy in copies:
        copy.start()
    query = lax.broadcasted_iota(jnp.int32, (SEQ, SEQ), 0)
    key = lax.broadcasted_iota(jnp.int32, (SEQ, SEQ), 1)
    sequences = tokens // SEQ
    low = lax.broadcasted_iota(jnp.int32, (SEQ, PAIR), 1) < HEAD_DIM
    zeros = jnp.zeros((SEQ, PAIR), BF16)
    ones = jnp.ones((SEQ, PAIR), BF16)

    def by_head(block):
        return jnp.concatenate([jnp.where(low, block, zeros), jnp.where(low, zeros, block)], 0)

    counts = by_head(0.5 * ones)
    chunk = width
    curve = math.sqrt(2 / math.pi)
    copies[0].wait()
    copies[1].wait()
    state[...] = begun[...]

    def substep(first):
        x = state[...]
        mean_square = jnp.mean(x * x, axis=1, keepdims=True)
        normed = (x * lax.rsqrt(mean_square + 1e-06) * scale[...]).astype(BF16)

        if first:
            copies[2].wait()

        for n in range(0, 3 * width, chunk):
            packed = jnp.dot(normed, w_in[:, n : n + chunk], preferred_element_type=F32)
            if n < width:
                packed = packed * QUERY_SCALE
            qkv[:, n : n + chunk] = packed.astype(BF16)

        if first:
            copies[3].wait()
            for s in range(sequences):
                allowed = (key <= query) & (key < limits[s])
                bias[pl.ds(s * SEQ, SEQ), :] = jnp.where(allowed, 0.0, -1e30).astype(F32)

        for s in range(sequences):
            rows = pl.ds(s * SEQ, SEQ)
            mask = bias[rows, :]
            masks = jnp.concatenate([mask, mask], 0)
            for at in range(0, width, PAIR):
                queries = qkv[rows, at : at + PAIR]
                keys = qkv[rows, width + at : width + at + PAIR]
                values = qkv[rows, 2 * width + at : 2 * width + at + PAIR]
                scores = lax.dot_general(
                    by_head(queries), keys, (((1,), (1,)), ((), ())), preferred_element_type=F32
                ) + masks
                top = jnp.max(scores, axis=-1, keepdims=True)
                weights = jnp.exp2(scores - top).astype(BF16)
                pair = jnp.concatenate([weights[:SEQ], weights[SEQ:]], 1)
                both = jnp.dot(
                    pair, jnp.concatenate([by_head(values), counts], 1), preferred_element_type=F32
                )
                act[rows, at : at + PAIR] = (both[:, :PAIR] / both[:, PAIR:]).astype(BF16)

        if first:
            copies[4].wait()

        for n in range(0, hidden, chunk):
            u = jnp.dot(
                normed, w_in[:, 3 * width + n : 3 * width + n + chunk], preferred_element_type=F32
            )
            gelu = u + u * jnp.tanh(u * (curve + (curve * 0.044715) * (u * u)))
            act[:, width + n : width + n + chunk] = gelu.astype(BF16)

        if first:
            copies[5].wait()
            copies[6].wait()

        state[...] = x + jnp.dot(act[...], w_back[...], preferred_element_type=F32) * (0.5 / FINE)

    substep(True)

    @pl.loop(1, FINE)
    def _(_):
        substep(False)

    copies[7].wait()
    layer, _ = place()
    share = jnp.where(layer == 0, 0.0, 1.0).astype(F32)
    high, low_part = halves_of(0.3 * varying[...])
    through = 0.9 * begun[...] + dot_split(begun[...], high, low_part)
    state[...] = state[...] - share * through
    mine = layer % 2
    half = pieces[0].shape[0]
    for at in range(len(pieces) // 2):
        for piece, part in ((pieces[2 * at], mine), (pieces[2 * at + 1], 1 - mine)):
            piece[...] = state[pl.ds(pl.multiple_of((2 * at + part) * half, half), half), :]


def fine_jump(chunks, lengths, start, gain, surrogate, w_qkv, w_out, w_up, w_down):
    tokens, width = start.shape[1:]
    hidden = w_up.shape[2]
    half = jax.ShapeDtypeStruct((tokens // (2 * chunks), width), F32)
    return pl.pallas_call(
        fine_kernel,
        in_specs=[in_place()] * 8,
        out_specs=[in_vmem()] * (2 * chunks),
        out_shape=[half] * (2 * chunks),
        scratch_shapes=[
            pltpu.VMEM((tokens, width), F32),
            pltpu.VMEM(gain.shape, F32),
            pltpu.SMEM(lengths.shape, jnp.int32),
            pltpu.VMEM((width, 3 * width + hidden), BF16),
            pltpu.VMEM((width + hidden, width), BF16),
            pltpu.VMEM((width, width), F32),
            pltpu.VMEM((tokens, width), F32),
            pltpu.VMEM((tokens, width + hidden), BF16),
            pltpu.VMEM((tokens, 3 * width), BF16),
            pltpu.VMEM((tokens, SEQ), F32),
            pltpu.SemaphoreType.DMA((8,)),
        ],
        cost_estimate=pl.CostEstimate(
            flops=2 * FINE * tokens * width * (4 * width + 2 * hidden),
            transcendentals=FINE * tokens * hidden,
            bytes_accessed=2 * width * (4 * width + 2 * hidden),
        ),
        compiler_params=params(62),
    )(lengths, start, gain, surrogate, w_qkv, w_out, w_up, w_down)


def partner_map(got, passed, other):
    core = lax.axis_index("dp") % 2

    @pl.when(core == 0)
    def _():
        other[...] = 0.3 * got[0]

    @pl.when(core != 0)
    def _():
        other[...] = 0.3 * passed[0]


def odd_kernel(own, got, passed, odd_high, odd_low, other):
    even = is_even()

    @pl.when(even)
    def _():
        partner_map(got, passed, other)

    @pl.when(jnp.logical_not(even))
    def _():
        other[...] = 0.3 * own[0]

    odd_high[...], odd_low[...] = halves_of(other[...])


def odd_map(own, got, passed):
    width = own.shape[1]
    square = jax.ShapeDtypeStruct((width, width), BF16)
    return pl.pallas_call(
        odd_kernel,
        in_specs=[in_vmem()] * 3,
        out_specs=[in_vmem()] * 2,
        out_shape=[square] * 2,
        scratch_shapes=[pltpu.VMEM((width, width), F32)],
        compiler_params=params(8),
    )(own, got, passed)


def maps_kernel(
    own, got, passed, odd_high, odd_low, own_high, own_low, even_high, even_low, both_high, both_low, other
):
    even = is_even()

    @pl.when(even)
    def _():
        other[...] = 0.3 * own[0]

    @pl.when(jnp.logical_not(even))
    def _():
        partner_map(got, passed, other)

    own_high[...], own_low[...] = halves_of(0.3 * own[0])
    first = other[...]
    even_high[...], even_low[...] = halves_of(first)
    second = odd_high[...].astype(F32) + odd_low[...].astype(F32)
    product = 0.9 * (first + second) + dot_split(first, odd_high[...], odd_low[...])
    both_high[...], both_low[...] = halves_of(product)


def maps(own, got, passed, odd):
    width = own.shape[1]
    square = jax.ShapeDtypeStruct((width, width), BF16)
    return pl.pallas_call(
        maps_kernel,
        in_specs=[in_vmem()] * 5,
        out_specs=[in_vmem()] * 6,
        out_shape=[square] * 6,
        scratch_shapes=[pltpu.VMEM((width, width), F32)],
        compiler_params=params(14),
    )(own, got, passed, *odd)


def join_kernel(kept, received, odd_high, odd_low, out):
    even = is_even()
    first = jnp.where(even, kept[...], received[...])
    second = jnp.where(even, received[...], kept[...])
    out[...] = second + (0.9 * first + dot_split(first, odd_high[...], odd_low[...]))


def join(kept, received, odd):
    return pl.pallas_call(
        join_kernel,
        in_specs=[in_vmem()] * 4,
        out_specs=in_vmem(),
        out_shape=jax.ShapeDtypeStruct(kept.shape, F32),
        compiler_params=params(8),
    )(kept, received, *odd)


def hop_kernel(incoming, joined, both_high, both_low, out):
    state = incoming[...]
    out[...] = joined[...] + (0.81 * state + dot_split(state, both_high[...], both_low[...]))


def hop(incoming, joined, both):
    return pl.pallas_call(
        hop_kernel,
        in_specs=[in_vmem()] * 4,
        out_specs=in_vmem(),
        out_shape=jax.ShapeDtypeStruct(incoming.shape, F32),
        compiler_params=params(8),
    )(incoming, joined, *both)


def turn_kernel(kept, received, even_high, even_low, *arrivals_and_outs):
    *arrivals, head, out = arrivals_and_outs
    state = functools.reduce(jnp.add, [arrival[...] for arrival in arrivals])
    even = is_even()
    first = jnp.where(even, kept[...], received[...])
    after = first + (0.9 * state + dot_split(state, even_high[...], even_low[...]))
    head[...] = jnp.where(even, state, after)
    out[...] = jnp.where(even, after, state)


def turn(kept, received, even, arrivals):
    shape = jax.ShapeDtypeStruct(kept.shape, F32)
    return pl.pallas_call(
        turn_kernel,
        in_specs=[in_vmem()] * (4 + len(arrivals)),
        out_specs=[in_vmem()] * 2,
        out_shape=[shape, shape],
        compiler_params=params(8),
    )(kept, received, *even, *arrivals)


def part_of(row, ahead, jump, start, own_high, own_low):
    half, width = ahead.shape
    state = ahead[...]
    new = jump[...] + (0.9 * state + dot_split(state, own_high[...], own_low[...]))
    difference = state - start[0, pl.ds(pl.multiple_of(row * half, half), half), :]
    total = lax.dot_general(
        jnp.ones((8, width), F32), difference * difference, (((1,), (1,)), ((), ())),
        precision=lax.Precision.HIGHEST, preferred_element_type=F32,
    )
    return new, jnp.sqrt(total * (1.0 / width))


def part_kernel(at, other, ahead, jump, start, own_high, own_low, new, change):
    row = 2 * at + (lax.axis_index("layer") + other) % 2
    new[...], change[...] = part_of(row, ahead, jump, start, own_high, own_low)


def part(at, other, ahead, jump, start, own):
    half, width = ahead.shape
    return pl.pallas_call(
        functools.partial(part_kernel, at, other),
        in_specs=[in_vmem()] * 5,
        out_specs=[in_vmem()] * 2,
        out_shape=[
            jax.ShapeDtypeStruct((half, width), F32), jax.ShapeDtypeStruct((8, half), F32)
        ],
        compiler_params=params(8),
    )(ahead, jump, start, *own)


def close_kernel(count, ahead, jump, start, own_high, own_low, *rest):
    *done, out, change = rest
    half = ahead.shape[0]
    layer = lax.axis_index("layer")
    even = layer % 2 == 0
    share = jnp.where(layer == 0, 0.0, 1.0).astype(F32)
    last = part_of(2 * count - 1 - layer % 2, ahead, jump, start, own_high, own_low)
    done = [(done[at][...], done[at + 1][...]) for at in range(0, len(done), 2)] + [last]
    for at in range(count):
        (mine, mine_change), (other, other_change) = done[2 * at], done[2 * at + 1]
        out[0, pl.ds(2 * at * half, half), :] = jnp.where(even, mine, other)
        out[0, pl.ds((2 * at + 1) * half, half), :] = jnp.where(even, other, mine)
        row = jnp.where(
            even,
            jnp.concatenate([mine_change, other_change], 1),
            jnp.concatenate([other_change, mine_change], 1),
        )
        change[:, pl.ds(2 * at * half, 2 * half)] = share * row[:1]


def close(count, ahead, jump, start, own, done):
    tokens, width = start.shape[1:]
    return pl.pallas_call(
        functools.partial(close_kernel, count),
        in_specs=[in_vmem()] * (5 + len(done)),
        out_specs=[in_vmem()] * 2,
        out_shape=[
            jax.ShapeDtypeStruct((1, tokens, width), F32),
            jax.ShapeDtypeStruct((1, tokens), F32),
        ],
        compiler_params=params(12),
    )(ahead, jump, start, *own, *done)


def shards(old_heads, surrogate, norm_gain, w_qkv, w_out, w_up, w_down, lengths):
    layers = lax.axis_size("layer")
    batches = lax.axis_size("dp")
    partners = [(i, i ^ 1) for i in range(layers)]
    ports = [
        (i * batches + j, (i ^ 1) * batches + j) for i in range(layers) for j in range(0, batches, 2)
    ]
    got = lax.ppermute(surrogate, ("layer", "dp"), ports)
    pieces = fine_jump(CHUNKS, lengths, old_heads, norm_gain, surrogate, w_qkv, w_out, w_up, w_down)
    kept, sent = pieces[::2], pieces[1::2]
    spans = range(CHUNKS)
    received = []
    for c in spans:
        received.append(lax.ppermute(sent[c], "layer", partners))
    passed = lax.ppermute(got, "dp", [(i, i + 1) for i in range(0, batches - 1, 2)])
    odd = odd_map(surrogate, got, passed)
    split = maps(surrogate, got, passed, odd)
    own, even, both = split[0:2], split[2:4], split[4:6]
    joined = [join(kept[c], received[c], odd) for c in spans]
    carried = joined
    arrivals = [[] for c in spans]
    for at in range(0, layers - 2, 2):
        route = [(at, at + 2), (at + 1, at + 3)]
        for c in spans:
            arrivals[c].append(lax.ppermute(carried[c], "layer", route))
        if at < layers - 4:
            carried = [hop(arrivals[c][-1], joined[c], both) for c in spans]
    heads, returned = [], []
    for c in spans:
        head, out = turn(kept[c], received[c], even, arrivals[c])
        heads.append(head)
        returned.append(lax.ppermute(out, "layer", partners))
    done = []
    for c in spans:
        done += part(c, 0, heads[c], kept[c], old_heads, own)
        if c + 1 < CHUNKS:
            done += part(c, 1, returned[c], sent[c], old_heads, own)
    return close(CHUNKS, returned[-1], sent[-1], old_heads, own, done)


def solution(mesh):
    in_specs = (
        P("layer", "dp", None),
        P("layer", None, None),
        P("layer", None),
        P("layer", None, None),
        P("layer", None, None),
        P("layer", None, None),
        P("layer", None, None),
        P("dp"),
    )
    out_specs = (P("layer", "dp", None), P("layer", "dp"))
    return jax.shard_map(shards, mesh=mesh, in_specs=in_specs, out_specs=out_specs, check_vma=False)
```

```python
import functools
import math

import jax
import jax.numpy as jnp
from jax import lax
from jax.experimental import pallas as pl
from jax.experimental.pallas import tpu as pltpu
from jax.sharding import PartitionSpec as P


HEAD_DIM = 64
SEQ = 128
FINE = 4
QUERY_SCALE = math.log2(math.e) / math.sqrt(HEAD_DIM)
CHUNKS = 2
PAIR = 2 * HEAD_DIM
F32 = jnp.float32
BF16 = jnp.bfloat16


def halves_of(a):
    high = a.astype(BF16)
    return high, (a - high.astype(F32)).astype(BF16)


def dot_split(a, b_high, b_low):
    a_high, a_low = halves_of(a)
    rows = a.shape[0]
    both = jnp.dot(jnp.concatenate([a_high, a_low], 0), b_high, preferred_element_type=F32)
    return both[:rows] + (both[rows:] + jnp.dot(a_high, b_low, preferred_element_type=F32))


def params(megabytes):
    return pltpu.CompilerParams(vmem_limit_bytes=megabytes << 20)


def in_vmem():
    return pl.BlockSpec(memory_space=pltpu.VMEM)


def in_place():
    return pl.BlockSpec(memory_space=pltpu.HBM)


def is_even():
    return lax.axis_index("layer") % 2 == 0


def fine_kernel(
    lengths, start, gain, surrogate, w_qkv, w_out, w_up, w_down, *outs_and_scratch
):
    (
        *pieces, own_high, own_low, begun, scale, limits, w_in, w_back, varying, through,
        state, act, qkv, bias, sems,
    ) = outs_and_scratch
    tokens, width = state.shape
    hidden = w_back.shape[0] - width
    moves = (
        (start.at[0], begun),
        (gain, scale),
        (w_qkv.at[0], w_in.at[:, pl.ds(0, 3 * width)]),
        (lengths, limits),
        (w_up.at[0], w_in.at[:, pl.ds(3 * width, hidden)]),
        (w_out.at[0], w_back.at[pl.ds(0, width), :]),
        (w_down.at[0], w_back.at[pl.ds(width, hidden), :]),
        (surrogate.at[0], varying),
    )
    copies = [
        pltpu.make_async_copy(source, target, sems.at[at])
        for at, (source, target) in enumerate(moves)
    ]
    for copy in copies:
        copy.start()
    query = lax.broadcasted_iota(jnp.int32, (SEQ, SEQ), 0)
    key = lax.broadcasted_iota(jnp.int32, (SEQ, SEQ), 1)
    sequences = tokens // SEQ
    low = lax.broadcasted_iota(jnp.int32, (SEQ, PAIR), 1) < HEAD_DIM
    zeros = jnp.zeros((SEQ, PAIR), BF16)
    ones = jnp.ones((SEQ, PAIR), BF16)

    def by_head(block):
        return jnp.concatenate([jnp.where(low, block, zeros), jnp.where(low, zeros, block)], 0)

    counts = by_head(0.5 * ones)
    chunk = width
    curve = math.sqrt(2 / math.pi)
    copies[0].wait()
    copies[1].wait()
    state[...] = begun[...]

    def substep(first):
        x = state[...]
        mean_square = jnp.mean(x * x, axis=1, keepdims=True)
        normed = (x * lax.rsqrt(mean_square + 1e-06) * scale[...]).astype(BF16)

        if first:
            copies[2].wait()

        for n in range(0, 3 * width, chunk):
            packed = jnp.dot(normed, w_in[:, n : n + chunk], preferred_element_type=F32)
            if n < width:
                packed = packed * QUERY_SCALE
            qkv[:, n : n + chunk] = packed.astype(BF16)

        if first:
            copies[3].wait()
            for s in range(sequences):
                allowed = (key <= query) & (key < limits[s])
                bias[pl.ds(s * SEQ, SEQ), :] = jnp.where(allowed, 0.0, -1e30).astype(F32)

        for s in range(sequences):
            rows = pl.ds(s * SEQ, SEQ)
            mask = bias[rows, :]
            masks = jnp.concatenate([mask, mask], 0)
            for at in range(0, width, PAIR):
                queries = qkv[rows, at : at + PAIR]
                keys = qkv[rows, width + at : width + at + PAIR]
                values = qkv[rows, 2 * width + at : 2 * width + at + PAIR]
                scores = lax.dot_general(
                    by_head(queries), keys, (((1,), (1,)), ((), ())), preferred_element_type=F32
                ) + masks
                top = jnp.max(scores, axis=-1, keepdims=True)
                weights = jnp.exp2(scores - top).astype(BF16)
                pair = jnp.concatenate([weights[:SEQ], weights[SEQ:]], 1)
                both = jnp.dot(
                    pair, jnp.concatenate([by_head(values), counts], 1), preferred_element_type=F32
                )
                act[rows, at : at + PAIR] = (both[:, :PAIR] / both[:, PAIR:]).astype(BF16)

        if first:
            copies[4].wait()

        for n in range(0, hidden, chunk):
            u = jnp.dot(
                normed, w_in[:, 3 * width + n : 3 * width + n + chunk], preferred_element_type=F32
            )
            gelu = u + u * jnp.tanh(u * (curve + (curve * 0.044715) * (u * u)))
            act[:, width + n : width + n + chunk] = gelu.astype(BF16)

        if first:
            copies[7].wait()
            own_high[...], own_low[...] = halves_of(0.3 * varying[...])
            through[...] = 0.9 * begun[...] + dot_split(begun[...], own_high[...], own_low[...])
            copies[5].wait()
            copies[6].wait()

        state[...] = x + jnp.dot(act[...], w_back[...], preferred_element_type=F32) * (0.5 / FINE)

    substep(True)

    @pl.loop(1, FINE)
    def _(_):
        substep(False)

    layer = lax.axis_index("layer")
    share = jnp.where(layer == 0, 0.0, 1.0).astype(F32)
    state[...] = state[...] - share * through[...]
    mine = layer % 2
    half = pieces[0].shape[0]
    for at in range(len(pieces) // 2):
        for piece, part in ((pieces[2 * at], mine), (pieces[2 * at + 1], 1 - mine)):
            piece[...] = state[pl.ds(pl.multiple_of((2 * at + part) * half, half), half), :]


def fine_jump(chunks, lengths, start, gain, surrogate, w_qkv, w_out, w_up, w_down):
    tokens, width = start.shape[1:]
    hidden = w_up.shape[2]
    half = jax.ShapeDtypeStruct((tokens // (2 * chunks), width), F32)
    square = jax.ShapeDtypeStruct((width, width), BF16)
    return pl.pallas_call(
        fine_kernel,
        in_specs=[in_place()] * 8,
        out_specs=[in_vmem()] * (2 * chunks + 2),
        out_shape=[half] * (2 * chunks) + [square] * 2,
        scratch_shapes=[
            pltpu.VMEM((tokens, width), F32),
            pltpu.VMEM(gain.shape, F32),
            pltpu.SMEM(lengths.shape, jnp.int32),
            pltpu.VMEM((width, 3 * width + hidden), BF16),
            pltpu.VMEM((width + hidden, width), BF16),
            pltpu.VMEM((width, width), F32),
            pltpu.VMEM((tokens, width), F32),
            pltpu.VMEM((tokens, width), F32),
            pltpu.VMEM((tokens, width + hidden), BF16),
            pltpu.VMEM((tokens, 3 * width), BF16),
            pltpu.VMEM((tokens, SEQ), F32),
            pltpu.SemaphoreType.DMA((8,)),
        ],
        cost_estimate=pl.CostEstimate(
            flops=2 * FINE * tokens * width * (4 * width + 2 * hidden),
            transcendentals=FINE * tokens * hidden,
            bytes_accessed=2 * width * (4 * width + 2 * hidden),
        ),
        compiler_params=params(32),
    )(*[pltpu.with_memory_space_constraint(a, pltpu.HBM) for a in (lengths, start, gain, surrogate, w_qkv, w_out, w_up, w_down)])


def other_kernel(got, passed, high, low):
    part = got.shape[0]
    core = lax.axis_index("dp") % 2
    for source, where in ((got, core), (passed, 1 - core)):
        rows = pl.ds(pl.multiple_of(where * part, part), part)
        high[rows, :], low[rows, :] = halves_of(0.3 * source[...])


def other_map(got, passed):
    part, width = got.shape
    square = jax.ShapeDtypeStruct((2 * part, width), BF16)
    return pl.pallas_call(
        other_kernel,
        in_specs=[in_vmem()] * 2,
        out_specs=[in_vmem()] * 2,
        out_shape=[square] * 2,
        compiler_params=params(6),
    )(got, passed)


def both_kernel(own_high, own_low, other_high, other_low, both_high, both_low):
    def product(first_high, first_low, second_high, second_low):
        a_high, a_low = first_high[...], first_low[...]
        b_high, b_low = second_high[...], second_low[...]
        total = (a_high.astype(F32) + b_high.astype(F32)) + (a_low.astype(F32) + b_low.astype(F32))
        dot = functools.partial(jnp.dot, preferred_element_type=F32)
        value = 0.9 * total + (dot(a_high, b_high) + (dot(a_low, b_high) + dot(a_high, b_low)))
        both_high[...], both_low[...] = halves_of(value)

    even = is_even()

    @pl.when(even)
    def _():
        product(own_high, own_low, other_high, other_low)

    @pl.when(jnp.logical_not(even))
    def _():
        product(other_high, other_low, own_high, own_low)


def both_map(own, other):
    return pl.pallas_call(
        both_kernel,
        in_specs=[in_vmem()] * 4,
        out_specs=[in_vmem()] * 2,
        out_shape=[jax.ShapeDtypeStruct(part.shape, BF16) for part in own],
        compiler_params=params(10),
    )(*own, *other)


def join_kernel(kept, received, own_high, own_low, other_high, other_low, out):
    even = is_even()

    @pl.when(even)
    def _():
        first = kept[...]
        out[...] = received[...] + (0.9 * first + dot_split(first, other_high[...], other_low[...]))

    @pl.when(jnp.logical_not(even))
    def _():
        first = received[...]
        out[...] = kept[...] + (0.9 * first + dot_split(first, own_high[...], own_low[...]))


def join(kept, received, own, other):
    return pl.pallas_call(
        join_kernel,
        in_specs=[in_vmem()] * 6,
        out_specs=in_vmem(),
        out_shape=jax.ShapeDtypeStruct(kept.shape, F32),
        compiler_params=params(8),
    )(kept, received, *own, *other)


def hop_kernel(incoming, joined, both_high, both_low, out):
    state = incoming[...]
    out[...] = joined[...] + (0.81 * state + dot_split(state, both_high[...], both_low[...]))


def hop(incoming, joined, both):
    return pl.pallas_call(
        hop_kernel,
        in_specs=[in_vmem()] * 4,
        out_specs=in_vmem(),
        out_shape=jax.ShapeDtypeStruct(incoming.shape, F32),
        compiler_params=params(8),
    )(incoming, joined, *both)


def turn_kernel(
    kept, received, own_high, own_low, other_high, other_low, *arrivals_and_outs
):
    *arrivals, head, out = arrivals_and_outs
    state = functools.reduce(jnp.add, [arrival[...] for arrival in arrivals])
    even = is_even()

    @pl.when(even)
    def _():
        head[...] = state
        out[...] = kept[...] + (0.9 * state + dot_split(state, own_high[...], own_low[...]))

    @pl.when(jnp.logical_not(even))
    def _():
        out[...] = state
        head[...] = received[...] + (0.9 * state + dot_split(state, other_high[...], other_low[...]))


def turn(kept, received, own, other, arrivals):
    shape = jax.ShapeDtypeStruct(kept.shape, F32)
    return pl.pallas_call(
        turn_kernel,
        in_specs=[in_vmem()] * (6 + len(arrivals)),
        out_specs=[in_vmem()] * 2,
        out_shape=[shape, shape],
        compiler_params=params(8),
    )(kept, received, *own, *other, *arrivals)


def part_of(row, ahead, jump, start, own_high, own_low):
    half, width = ahead.shape
    state = ahead[...]
    new = jump[...] + (0.9 * state + dot_split(state, own_high[...], own_low[...]))
    difference = state - start[0, pl.ds(pl.multiple_of(row * half, half), half), :]
    total = lax.dot_general(
        jnp.ones((8, width), F32), difference * difference, (((1,), (1,)), ((), ())),
        precision=lax.Precision.HIGHEST, preferred_element_type=F32,
    )
    return new, jnp.sqrt(total * (1.0 / width))


def part_kernel(at, other, ahead, jump, start, own_high, own_low, new, change):
    row = 2 * at + (lax.axis_index("layer") + other) % 2
    new[...], change[...] = part_of(row, ahead, jump, start, own_high, own_low)


def part(at, other, ahead, jump, start, own):
    half, width = ahead.shape
    return pl.pallas_call(
        functools.partial(part_kernel, at, other),
        in_specs=[in_vmem()] * 5,
        out_specs=[in_vmem()] * 2,
        out_shape=[
            jax.ShapeDtypeStruct((half, width), F32), jax.ShapeDtypeStruct((8, half), F32)
        ],
        compiler_params=params(8),
    )(ahead, jump, start, *own)


def close_kernel(count, ahead, jump, start, own_high, own_low, *rest):
    *done, out, change = rest
    half = ahead.shape[0]
    layer = lax.axis_index("layer")
    even = layer % 2 == 0
    share = jnp.where(layer == 0, 0.0, 1.0).astype(F32)
    last = part_of(2 * count - 1 - layer % 2, ahead, jump, start, own_high, own_low)
    done = [(done[at][...], done[at + 1][...]) for at in range(0, len(done), 2)] + [last]
    for at in range(count):
        (mine, mine_change), (other, other_change) = done[2 * at], done[2 * at + 1]
        out[0, pl.ds(2 * at * half, half), :] = jnp.where(even, mine, other)
        out[0, pl.ds((2 * at + 1) * half, half), :] = jnp.where(even, other, mine)
        row = jnp.where(
            even,
            jnp.concatenate([mine_change, other_change], 1),
            jnp.concatenate([other_change, mine_change], 1),
        )
        change[:, pl.ds(2 * at * half, 2 * half)] = share * row[:1]


def close(count, ahead, jump, start, own, done):
    tokens, width = start.shape[1:]
    return pl.pallas_call(
        functools.partial(close_kernel, count),
        in_specs=[in_vmem()] * (5 + len(done)),
        out_specs=[in_vmem()] * 2,
        out_shape=[
            jax.ShapeDtypeStruct((1, tokens, width), F32),
            jax.ShapeDtypeStruct((1, tokens), F32),
        ],
        compiler_params=params(12),
    )(ahead, jump, start, *own, *done)


def shards(old_heads, surrogate, norm_gain, w_qkv, w_out, w_up, w_down, lengths):
    layers = lax.axis_size("layer")
    batches = lax.axis_size("dp")
    partners = [(i, i ^ 1) for i in range(layers)]
    neighbours = [(i, i ^ 1) for i in range(batches)]
    half = surrogate.shape[1] // 2
    core = lax.axis_index("dp") % 2
    mine = lax.dynamic_slice_in_dim(surrogate[0], core * half, half, 0)
    got = lax.ppermute(mine, "layer", partners)
    *pieces, own_high, own_low = fine_jump(
        CHUNKS, lengths, old_heads, norm_gain, surrogate, w_qkv, w_out, w_up, w_down
    )
    own = own_high, own_low
    kept, sent = pieces[::2], pieces[1::2]
    spans = range(CHUNKS)
    received = []
    for c in spans:
        received.append(lax.ppermute(sent[c], "layer", partners))
    passed = lax.ppermute(got, "dp", neighbours)
    other = other_map(got, passed)
    both = both_map(own, other)
    joined = [join(kept[c], received[c], own, other) for c in spans]
    carried = joined
    arrivals = [[] for c in spans]
    for at in range(0, layers - 2, 2):
        route = [(at, at + 2), (at + 1, at + 3)]
        for c in spans:
            arrivals[c].append(lax.ppermute(carried[c], "layer", route))
        if at < layers - 4:
            carried = [hop(arrivals[c][-1], joined[c], both) for c in spans]
    heads, returned = [], []
    for c in spans:
        head, out = turn(kept[c], received[c], own, other, arrivals[c])
        heads.append(head)
        returned.append(lax.ppermute(out, "layer", partners))
    done = []
    for c in spans:
        done += part(c, 0, heads[c], kept[c], old_heads, own)
        if c + 1 < CHUNKS:
            done += part(c, 1, returned[c], sent[c], old_heads, own)
    return close(CHUNKS, returned[-1], sent[-1], old_heads, own, done)


def solution(mesh):
    in_specs = (
        P("layer", "dp", None),
        P("layer", None, None),
        P("layer", None),
        P("layer", None, None),
        P("layer", None, None),
        P("layer", None, None),
        P("layer", None, None),
        P("dp"),
    )
    out_specs = (P("layer", "dp", None), P("layer", "dp"))
    return jax.shard_map(shards, mesh=mesh, in_specs=in_specs, out_specs=out_specs, check_vma=False)
```

```python
import functools
import math

import jax
import jax.numpy as jnp
from jax import lax
from jax.experimental import pallas as pl
from jax.experimental.pallas import tpu as pltpu
from jax.sharding import PartitionSpec as P


HEAD_DIM = 64
SEQ = 128
FINE = 4
QUERY_SCALE = math.log2(math.e) / math.sqrt(HEAD_DIM)
CHUNKS = 2
PAIR = 2 * HEAD_DIM
F32 = jnp.float32
BF16 = jnp.bfloat16


def halves_of(a):
    high = a.astype(BF16)
    return high, (a - high.astype(F32)).astype(BF16)


def dot_split(a, b_high, b_low):
    a_high, a_low = halves_of(a)
    rows = a.shape[0]
    both = jnp.dot(jnp.concatenate([a_high, a_low], 0), b_high, preferred_element_type=F32)
    return both[:rows] + (both[rows:] + jnp.dot(a_high, b_low, preferred_element_type=F32))


def params(megabytes):
    return pltpu.CompilerParams(vmem_limit_bytes=megabytes << 20)


def in_vmem():
    return pl.BlockSpec(memory_space=pltpu.VMEM)


def in_place():
    return pl.BlockSpec(memory_space=pltpu.HBM)


def is_even():
    return lax.axis_index("layer") % 2 == 0


def fine_kernel(
    lengths, start, gain, surrogate, w_qkv, w_out, w_up, w_down, *outs_and_scratch
):
    (
        *pieces, own_high, own_low, begun, scale, limits, w_in, w_back, varying, through,
        state, act, qkv, bias, sems,
    ) = outs_and_scratch
    tokens, width = state.shape
    hidden = w_back.shape[0] - width
    moves = (
        (start.at[0], begun),
        (gain, scale),
        (w_qkv.at[0], w_in.at[:, pl.ds(0, 3 * width)]),
        (lengths, limits),
        (w_up.at[0], w_in.at[:, pl.ds(3 * width, hidden)]),
        (w_out.at[0], w_back.at[pl.ds(0, width), :]),
        (w_down.at[0], w_back.at[pl.ds(width, hidden), :]),
        (surrogate.at[0], varying),
    )
    copies = [
        pltpu.make_async_copy(source, target, sems.at[at])
        for at, (source, target) in enumerate(moves)
    ]
    for copy in copies:
        copy.start()
    query = lax.broadcasted_iota(jnp.int32, (SEQ, SEQ), 0)
    key = lax.broadcasted_iota(jnp.int32, (SEQ, SEQ), 1)
    sequences = tokens // SEQ
    low = lax.broadcasted_iota(jnp.int32, (SEQ, PAIR), 1) < HEAD_DIM
    zeros = jnp.zeros((SEQ, PAIR), BF16)
    ones = jnp.ones((SEQ, PAIR), BF16)

    def by_head(block):
        return jnp.concatenate([jnp.where(low, block, zeros), jnp.where(low, zeros, block)], 0)

    counts = by_head(0.5 * ones)
    chunk = width
    curve = math.sqrt(2 / math.pi)
    copies[0].wait()
    copies[1].wait()
    state[...] = begun[...]

    def substep(first):
        x = state[...]
        mean_square = jnp.mean(x * x, axis=1, keepdims=True)
        normed = (x * lax.rsqrt(mean_square + 1e-06) * scale[...]).astype(BF16)

        if first:
            copies[2].wait()

        for n in range(0, 3 * width, chunk):
            packed = jnp.dot(normed, w_in[:, n : n + chunk], preferred_element_type=F32)
            if n < width:
                packed = packed * QUERY_SCALE
            qkv[:, n : n + chunk] = packed.astype(BF16)

        if first:
            copies[3].wait()
            for s in range(sequences):
                allowed = (key <= query) & (key < limits[s])
                bias[pl.ds(s * SEQ, SEQ), :] = jnp.where(allowed, 0.0, -1e30).astype(F32)

        for s in range(sequences):
            rows = pl.ds(s * SEQ, SEQ)
            mask = bias[rows, :]
            masks = jnp.concatenate([mask, mask], 0)
            for at in range(0, width, PAIR):
                queries = qkv[rows, at : at + PAIR]
                keys = qkv[rows, width + at : width + at + PAIR]
                values = qkv[rows, 2 * width + at : 2 * width + at + PAIR]
                scores = lax.dot_general(
                    by_head(queries), keys, (((1,), (1,)), ((), ())), preferred_element_type=F32
                ) + masks
                top = jnp.max(scores, axis=-1, keepdims=True)
                weights = jnp.exp2(scores - top).astype(BF16)
                pair = jnp.concatenate([weights[:SEQ], weights[SEQ:]], 1)
                both = jnp.dot(
                    pair, jnp.concatenate([by_head(values), counts], 1), preferred_element_type=F32
                )
                act[rows, at : at + PAIR] = (both[:, :PAIR] / both[:, PAIR:]).astype(BF16)

        if first:
            copies[4].wait()

        for n in range(0, hidden, chunk):
            u = jnp.dot(
                normed, w_in[:, 3 * width + n : 3 * width + n + chunk], preferred_element_type=F32
            )
            gelu = u + u * jnp.tanh(u * (curve + (curve * 0.044715) * (u * u)))
            act[:, width + n : width + n + chunk] = gelu.astype(BF16)

        if first:
            copies[7].wait()
            own_high[...], own_low[...] = halves_of(0.3 * varying[...])
            through[...] = 0.9 * begun[...] + dot_split(begun[...], own_high[...], own_low[...])
            copies[5].wait()
            copies[6].wait()

        state[...] = x + jnp.dot(act[...], w_back[...], preferred_element_type=F32) * (0.5 / FINE)

    substep(True)

    @pl.loop(1, FINE)
    def _(_):
        substep(False)

    layer = lax.axis_index("layer")
    share = jnp.where(layer == 0, 0.0, 1.0).astype(F32)
    state[...] = state[...] - share * through[...]
    mine = layer % 2
    half = pieces[0].shape[0]
    for at in range(len(pieces) // 2):
        for piece, part in ((pieces[2 * at], mine), (pieces[2 * at + 1], 1 - mine)):
            piece[...] = state[pl.ds(pl.multiple_of((2 * at + part) * half, half), half), :]


def fine_jump(chunks, lengths, start, gain, surrogate, w_qkv, w_out, w_up, w_down):
    tokens, width = start.shape[1:]
    hidden = w_up.shape[2]
    half = jax.ShapeDtypeStruct((tokens // (2 * chunks), width), F32)
    square = jax.ShapeDtypeStruct((width, width), BF16)
    return pl.pallas_call(
        fine_kernel,
        in_specs=[in_place()] * 8,
        out_specs=[in_vmem()] * (2 * chunks + 2),
        out_shape=[half] * (2 * chunks) + [square] * 2,
        scratch_shapes=[
            pltpu.VMEM((tokens, width), F32),
            pltpu.VMEM(gain.shape, F32),
            pltpu.SMEM(lengths.shape, jnp.int32),
            pltpu.VMEM((width, 3 * width + hidden), BF16),
            pltpu.VMEM((width + hidden, width), BF16),
            pltpu.VMEM((width, width), F32),
            pltpu.VMEM((tokens, width), F32),
            pltpu.VMEM((tokens, width), F32),
            pltpu.VMEM((tokens, width + hidden), BF16),
            pltpu.VMEM((tokens, 3 * width), BF16),
            pltpu.VMEM((tokens, SEQ), F32),
            pltpu.SemaphoreType.DMA((8,)),
        ],
        cost_estimate=pl.CostEstimate(
            flops=2 * FINE * tokens * width * (4 * width + 2 * hidden),
            transcendentals=FINE * tokens * hidden,
            bytes_accessed=2 * width * (4 * width + 2 * hidden),
        ),
        compiler_params=params(32),
    )(*[pltpu.with_memory_space_constraint(a, pltpu.HBM) for a in (lengths, start, gain, surrogate, w_qkv, w_out, w_up, w_down)])


def other_kernel(got, passed, high, low):
    part = got.shape[0]
    core = lax.axis_index("dp") % 2
    for source, where in ((got, core), (passed, 1 - core)):
        rows = pl.ds(pl.multiple_of(where * part, part), part)
        high[rows, :], low[rows, :] = halves_of(0.3 * source[...])


def other_map(got, passed):
    part, width = got.shape
    square = jax.ShapeDtypeStruct((2 * part, width), BF16)
    return pl.pallas_call(
        other_kernel,
        in_specs=[in_vmem()] * 2,
        out_specs=[in_vmem()] * 2,
        out_shape=[square] * 2,
        compiler_params=params(6),
    )(got, passed)


def both_kernel(own_high, own_low, other_high, other_low, both_high, both_low):
    def product(first_high, first_low, second_high, second_low):
        a_high, a_low = first_high[...], first_low[...]
        b_high, b_low = second_high[...], second_low[...]
        total = (a_high.astype(F32) + b_high.astype(F32)) + (a_low.astype(F32) + b_low.astype(F32))
        dot = functools.partial(jnp.dot, preferred_element_type=F32)
        value = 0.9 * total + (dot(a_high, b_high) + (dot(a_low, b_high) + dot(a_high, b_low)))
        both_high[...], both_low[...] = halves_of(value)

    even = is_even()

    @pl.when(even)
    def _():
        product(own_high, own_low, other_high, other_low)

    @pl.when(jnp.logical_not(even))
    def _():
        product(other_high, other_low, own_high, own_low)


def both_map(own, other):
    return pl.pallas_call(
        both_kernel,
        in_specs=[in_vmem()] * 4,
        out_specs=[in_vmem()] * 2,
        out_shape=[jax.ShapeDtypeStruct(part.shape, BF16) for part in own],
        compiler_params=params(10),
    )(*own, *other)


def join_kernel(kept, received, own_high, own_low, other_high, other_low, out):
    even = is_even()

    @pl.when(even)
    def _():
        first = kept[...]
        out[...] = received[...] + (0.9 * first + dot_split(first, other_high[...], other_low[...]))

    @pl.when(jnp.logical_not(even))
    def _():
        first = received[...]
        out[...] = kept[...] + (0.9 * first + dot_split(first, own_high[...], own_low[...]))


def join(kept, received, own, other):
    return pl.pallas_call(
        join_kernel,
        in_specs=[in_vmem()] * 6,
        out_specs=in_vmem(),
        out_shape=jax.ShapeDtypeStruct(kept.shape, F32),
        compiler_params=params(8),
    )(kept, received, *own, *other)


def hop_kernel(incoming, joined, both_high, both_low, out):
    state = incoming[...]
    out[...] = joined[...] + (0.81 * state + dot_split(state, both_high[...], both_low[...]))


def hop(incoming, joined, both):
    return pl.pallas_call(
        hop_kernel,
        in_specs=[in_vmem()] * 4,
        out_specs=in_vmem(),
        out_shape=jax.ShapeDtypeStruct(incoming.shape, F32),
        compiler_params=params(8),
    )(incoming, joined, *both)


def turn_kernel(
    kept, received, own_high, own_low, other_high, other_low, *arrivals_and_outs
):
    *arrivals, head, out = arrivals_and_outs
    state = functools.reduce(jnp.add, [arrival[...] for arrival in arrivals])
    even = is_even()

    @pl.when(even)
    def _():
        head[...] = state
        out[...] = kept[...] + (0.9 * state + dot_split(state, own_high[...], own_low[...]))

    @pl.when(jnp.logical_not(even))
    def _():
        out[...] = state
        head[...] = received[...] + (0.9 * state + dot_split(state, other_high[...], other_low[...]))


def turn(kept, received, own, other, arrivals):
    shape = jax.ShapeDtypeStruct(kept.shape, F32)
    return pl.pallas_call(
        turn_kernel,
        in_specs=[in_vmem()] * (6 + len(arrivals)),
        out_specs=[in_vmem()] * 2,
        out_shape=[shape, shape],
        compiler_params=params(8),
    )(kept, received, *own, *other, *arrivals)


def part_of(row, ahead, jump, start, own_high, own_low):
    half, width = ahead.shape
    state = ahead[...]
    new = jump[...] + (0.9 * state + dot_split(state, own_high[...], own_low[...]))
    difference = state - start[0, pl.ds(pl.multiple_of(row * half, half), half), :]
    ones = jnp.ones((8, width), BF16)
    total = sum(
        lax.dot_general(ones, square, (((1,), (1,)), ((), ())), preferred_element_type=F32)
        for square in halves_of(difference * difference)
    )
    return new, jnp.sqrt(total * (1.0 / width))


def part_kernel(at, other, ahead, jump, start, own_high, own_low, new, change):
    row = 2 * at + (lax.axis_index("layer") + other) % 2
    new[...], change[...] = part_of(row, ahead, jump, start, own_high, own_low)


def part(at, other, ahead, jump, start, own):
    half, width = ahead.shape
    return pl.pallas_call(
        functools.partial(part_kernel, at, other),
        in_specs=[in_vmem()] * 5,
        out_specs=[in_vmem()] * 2,
        out_shape=[
            jax.ShapeDtypeStruct((half, width), F32), jax.ShapeDtypeStruct((8, half), F32)
        ],
        compiler_params=params(8),
    )(ahead, jump, start, *own)


def close_kernel(count, ahead, jump, start, own_high, own_low, *rest):
    *done, out, change = rest
    half = ahead.shape[0]
    layer = lax.axis_index("layer")
    even = layer % 2 == 0
    share = jnp.where(layer == 0, 0.0, 1.0).astype(F32)
    last = part_of(2 * count - 1 - layer % 2, ahead, jump, start, own_high, own_low)
    done = [(done[at][...], done[at + 1][...]) for at in range(0, len(done), 2)] + [last]
    for at in range(count):
        (mine, mine_change), (other, other_change) = done[2 * at], done[2 * at + 1]
        out[0, pl.ds(2 * at * half, half), :] = jnp.where(even, mine, other)
        out[0, pl.ds((2 * at + 1) * half, half), :] = jnp.where(even, other, mine)
        row = jnp.where(
            even,
            jnp.concatenate([mine_change, other_change], 1),
            jnp.concatenate([other_change, mine_change], 1),
        )
        change[:, pl.ds(2 * at * half, 2 * half)] = share * row[:1]


def close(count, ahead, jump, start, own, done):
    tokens, width = start.shape[1:]
    return pl.pallas_call(
        functools.partial(close_kernel, count),
        in_specs=[in_vmem()] * (5 + len(done)),
        out_specs=[in_vmem()] * 2,
        out_shape=[
            jax.ShapeDtypeStruct((1, tokens, width), F32),
            jax.ShapeDtypeStruct((1, tokens), F32),
        ],
        compiler_params=params(12),
    )(ahead, jump, start, *own, *done)


def shards(old_heads, surrogate, norm_gain, w_qkv, w_out, w_up, w_down, lengths):
    layers = lax.axis_size("layer")
    batches = lax.axis_size("dp")
    partners = [(i, i ^ 1) for i in range(layers)]
    neighbours = [(i, i ^ 1) for i in range(batches)]
    half = surrogate.shape[1] // 2
    core = lax.axis_index("dp") % 2
    mine = lax.dynamic_slice_in_dim(surrogate[0], core * half, half, 0)
    got = lax.ppermute(mine, "layer", partners)
    *pieces, own_high, own_low = fine_jump(
        CHUNKS, lengths, old_heads, norm_gain, surrogate, w_qkv, w_out, w_up, w_down
    )
    own = own_high, own_low
    kept, sent = pieces[::2], pieces[1::2]
    spans = range(CHUNKS)
    received = []
    for c in spans:
        received.append(lax.ppermute(sent[c], "layer", partners))
    passed = lax.ppermute(got, "dp", neighbours)
    other = other_map(got, passed)
    both = both_map(own, other)
    joined = [join(kept[c], received[c], own, other) for c in spans]
    carried = joined
    arrivals = [[] for c in spans]
    for at in range(0, layers - 2, 2):
        route = [(at, at + 2), (at + 1, at + 3)]
        for c in spans:
            arrivals[c].append(lax.ppermute(carried[c], "layer", route))
        if at < layers - 4:
            carried = [hop(arrivals[c][-1], joined[c], both) for c in spans]
    heads, returned = [], []
    for c in spans:
        head, out = turn(kept[c], received[c], own, other, arrivals[c])
        heads.append(head)
        returned.append(lax.ppermute(out, "layer", partners))
    done = []
    for c in spans:
        done += part(c, 0, heads[c], kept[c], old_heads, own)
        if c + 1 < CHUNKS:
            done += part(c, 1, returned[c], sent[c], old_heads, own)
    return close(CHUNKS, returned[-1], sent[-1], old_heads, own, done)


def solution(mesh):
    in_specs = (
        P("layer", "dp", None),
        P("layer", None, None),
        P("layer", None),
        P("layer", None, None),
        P("layer", None, None),
        P("layer", None, None),
        P("layer", None, None),
        P("dp"),
    )
    out_specs = (P("layer", "dp", None), P("layer", "dp"))
    return jax.shard_map(shards, mesh=mesh, in_specs=in_specs, out_specs=out_specs, check_vma=False)
```
